32 devices in a mesh: space: 8 (over y, x, core), mode: 4 (over z).
Axes of the slice: x: 2, y: 2, z: 4, core: 2. Of those that a mesh axis runs over, the one named last changes fastest.
Arguments:
- start_modes: float32 [256, 24576], P('mode', 'space')
- hessian: bfloat16 [128, 8, 192, 192], P('space'), may hold values from -0.15625 to 0.15625
- block_exponent: int32 [128, 8], P('space'), may hold values from -1 to 1
- col_block: int32 [128, 8], P('space'), may hold values from 0 to 19, as said below
- grain_count: int32 [8], P('space'), may hold values from 384 to 512, as said below
Outputs:
- modes: float32 [256, 24576], P('mode', 'space')
The draws below stay inside these ranges and needn't reach their ends.
Inputs may be any that keep to these rules, and one draw needn't show every extreme that they name: col_block[b, k] lies between b mod 16 and b mod 16 + 2 * 2; slot 0 is b mod 16 + 2; both ends are reached in every slab. `grain_count`: at most 512 grains a slab, reached by at least one slab.
All inputs are finite; a program needn't handle non-finite values.
Results may differ from the reference program's by a relative error of at most 0.0034.
Values may be sent and summed in bfloat16 or wider, within the bound.
A program may use at most 64 MiB of HBM per device.

```python
import jax
import jax.numpy as jnp
from jax import lax

BLOCK = 192
MODES = 256
SLAB_BLOCKS = 16
CONTACTS = 8
HALO_BLOCKS = 2
ROWS = 3072
DOFS = 24576
TOTAL_BLOCKS = 128
N_SPACE = 8
N_MODE = 4


def draw_start_modes(key, part):
    columns = SLAB_BLOCKS * BLOCK * N_SPACE
    slabs = jnp.arange(columns, dtype=jnp.int32) // (SLAB_BLOCKS * BLOCK)
    rising = 1.0 + 2.0 * slabs.astype(jnp.float32) / max(N_SPACE - 1, 1)
    base = jax.random.normal(key, (MODES, columns), jnp.float32)
    return base * rising[None, :]


def draw_col_block(key, part):
    row_place = (jnp.arange(SLAB_BLOCKS * N_SPACE, dtype=jnp.int32) % SLAB_BLOCKS)[:, None]
    slot = jnp.arange(CONTACTS, dtype=jnp.int32)[None, :]
    offsets = jax.random.randint(key, (SLAB_BLOCKS * N_SPACE, CONTACTS), 0, 2 * HALO_BLOCKS + 1, jnp.int32)
    columns = row_place + offsets
    columns = jnp.where(slot == 0, row_place + HALO_BLOCKS, columns)
    columns = jnp.where((row_place == 0) & (slot == 1), 0, columns)
    columns = jnp.where((row_place == SLAB_BLOCKS - 1) & (slot == CONTACTS - 1), SLAB_BLOCKS - 1 + 2 * HALO_BLOCKS, columns)
    return columns.astype(jnp.int32)


def draw_grain_count(key, part):
    most = SLAB_BLOCKS * BLOCK // 6
    first_key, second_key = jax.random.split(key)
    counts = jax.random.randint(first_key, (N_SPACE,), most * 3 // 4, most + 1, jnp.int32)
    chosen = jax.random.randint(second_key, (), 0, N_SPACE, jnp.int32)
    return jnp.where(jnp.arange(N_SPACE, dtype=jnp.int32) == chosen, most, counts).astype(jnp.int32)


def with_ends(array, key, least, largest):
    spot = [jax.random.randint(jax.random.fold_in(key, axis), (), 0, length) for axis, length in enumerate(array.shape)]
    widest = array.shape.index(max(array.shape))
    next_to = spot[:widest] + [(spot[widest] + 1) % array.shape[widest]] + spot[widest + 1:]
    return array.at[tuple(spot)].set(least).at[tuple(next_to)].set(largest)


def block_levels(own_key, dims, cuts, smallest, largest):
    def one(dim, shards_of):
        steps = jax.random.uniform(jax.random.fold_in(jax.random.fold_in(own_key, 6), dim), (shards_of,), jnp.float32, smallest / len(cuts), largest / len(cuts))
        return jnp.repeat(jnp.exp(steps), dims[dim] // shards_of).reshape((-1,) + (1,) * (len(dims) - dim - 1))

    level = one(*cuts[0])
    for cut in cuts[1:]:
        level = level * one(*cut)
    return level


def bell_draw(rng, extent, spread, limit, cuts=(), kind=jnp.bfloat16):
    entries = spread * jax.random.normal(rng, extent, jnp.float32)
    if cuts:
        entries = entries * block_levels(rng, extent, cuts, -0.22, 0.18)
    return jnp.clip(entries, -limit, limit).astype(kind)


def setup_inputs(seed: int = 0) -> dict:
    arg_keys = jax.random.split(jax.random.key(seed), 6)
    start_modes = draw_start_modes(jax.random.fold_in(arg_keys[5], 71), 0)
    hessian = bell_draw(arg_keys[1], (TOTAL_BLOCKS, CONTACTS, BLOCK, BLOCK), (BLOCK * CONTACTS) ** -0.5, 0.15625, ((0, 8),))
    block_exponent = with_ends(jax.random.randint(arg_keys[2], (TOTAL_BLOCKS, CONTACTS), -1, 2), jax.random.fold_in(arg_keys[2], 1), -1, 1).astype(jnp.int32)
    col_block = draw_col_block(jax.random.fold_in(arg_keys[5], 71), 0)
    grain_count = draw_grain_count(jax.random.fold_in(arg_keys[5], 71), 0)
    return {"start_modes": start_modes, "hessian": hessian, "block_exponent": block_exponent, "col_block": col_block, "grain_count": grain_count}


filter_center = -0.5
filter_half = 1.5

def live_mask(grain_count):
    places = jnp.arange(DOFS, dtype=jnp.int32)
    slabs = places // ROWS
    inside = places % ROWS
    return (inside < 6 * grain_count[slabs]).astype(jnp.float32)

def operate(vectors_low, hessian, scales, global_cols):
    blocks_all = vectors_low.reshape(MODES, TOTAL_BLOCKS, BLOCK)

    def one_slab(slab_index):
        start = (slab_index * SLAB_BLOCKS).astype(jnp.int32)
        cols_here = lax.dynamic_slice_in_dim(global_cols, start, SLAB_BLOCKS, 0)
        scale_here = lax.dynamic_slice_in_dim(scales, start, SLAB_BLOCKS, 0)
        hess_here = lax.dynamic_slice_in_dim(hessian, start, SLAB_BLOCKS, 0)
        gathered = jnp.take(blocks_all, cols_here, axis=1).astype(jnp.float32)
        gathered = gathered * scale_here[None, :, :, None]
        return jnp.einsum('rkij,mrkj->mri', hess_here.astype(jnp.float32), gathered)
    parts = lax.map(one_slab, jnp.arange(N_SPACE, dtype=jnp.int32))
    return jnp.transpose(parts, (1, 0, 2, 3)).reshape(MODES, DOFS)

def reference(start_modes, hessian, block_exponent, col_block, grain_count):
    live = live_mask(grain_count)
    scales = jnp.exp2(block_exponent.astype(jnp.float32))
    slab_of_row = (jnp.arange(TOTAL_BLOCKS, dtype=jnp.int32) // SLAB_BLOCKS)[:, None]
    global_cols = ((slab_of_row * SLAB_BLOCKS - HALO_BLOCKS + col_block) % TOTAL_BLOCKS).astype(jnp.int32)
    start = start_modes * live
    image = operate(start.astype(jnp.bfloat16), hessian, scales, global_cols)
    first = (image - filter_center * start) / filter_half * live
    image = operate(first.astype(jnp.bfloat16), hessian, scales, global_cols)
    second = (2.0 * (image - filter_center * first) / filter_half - start) * live
    panel_size = MODES // N_MODE
    vectors = second
    for panel_index in range(N_MODE):
        low_edge = panel_index * panel_size
        high_edge = low_edge + panel_size
        panel = vectors[low_edge:high_edge]
        gram = jnp.dot(panel.astype(jnp.float32), panel.T.astype(jnp.float32), precision=lax.Precision.HIGHEST, preferred_element_type=jnp.float32)
        lower_factor = jnp.linalg.cholesky(gram)
        basis = jax.scipy.linalg.solve_triangular(lower_factor, panel, lower=True)
        later = vectors[high_edge:]
        coeffs = jnp.dot(later.astype(jnp.float32), basis.T.astype(jnp.float32), precision=lax.Precision.HIGHEST, preferred_element_type=jnp.float32)
        later = later - jnp.dot(coeffs.astype(jnp.float32), basis.astype(jnp.float32), precision=lax.Precision.HIGHEST, preferred_element_type=jnp.float32)
        vectors = jnp.concatenate([vectors[:low_edge], basis, later], axis=0)
    return vectors
```

```python
import functools

import jax
import jax.numpy as jnp
from jax import lax
from jax.experimental import pallas as pl
from jax.experimental.pallas import tpu as pltpu
from jax.sharding import PartitionSpec as P

HALO_BLOCKS = 2
GROUP = 2

filter_center = -0.5
filter_half = 1.5

F32 = jnp.float32
BF16 = jnp.bfloat16
MESH = pl.DeviceIdType.MESH
HIGHEST = lax.Precision.HIGHEST


def nt_dot(a, b, precision=None):
    return lax.dot_general(
        a, b, (((1,), (1,)), ((), ())), precision=precision, preferred_element_type=F32
    )


def filter_kernel(
    n_space, n_mode, exponent_ref, column_ref, count_ref, start_ref, hessian_ref,
    own_ref, panels_ref, gram_ref,
    hess, start, first, window_a, window_b, gacc, gsend, grecv, gz,
    hess_sem, halo_send, halo_recv, panel_send, panel_recv, rs_send, rs_recv,
    z_send, z_recv, ag_send, ag_recv,
):
    panel_size = start_ref.shape[0]
    slab_blocks, contacts, block, _ = hessian_ref.shape
    groups = slab_blocks // GROUP
    halo = HALO_BLOCKS
    share = panel_size // n_space
    here = lax.axis_index("space")
    level = lax.axis_index("mode")
    right = lax.rem(here + 1, n_space)
    left = lax.rem(here + n_space - 1, n_space)
    above = lax.rem(level + 1, n_mode)

    def hess_copy(b):
        return pltpu.make_async_copy(hessian_ref.at[b], hess.at[b], hess_sem.at[b])

    @pl.loop(0, slab_blocks)
    def _(i):
        hess_copy(lax.rem(i + slab_blocks - GROUP, slab_blocks)).start()

    barrier = pltpu.get_barrier_semaphore()
    for step in range(1, n_space):
        pl.semaphore_signal(barrier, inc=1, device_id={"space": lax.rem(here + step, n_space)}, device_id_type=MESH)
    for step in range(1, n_mode):
        pl.semaphore_signal(barrier, inc=1, device_id={"mode": lax.rem(level + step, n_mode)}, device_id_type=MESH)

    live_count = 6 * count_ref[0]

    def live_of(b):
        places = lax.broadcasted_iota(jnp.int32, (panel_size, block), 1) + b * block
        return (places < live_count).astype(F32)

    for b in range(slab_blocks):
        piece = start_ref[:, b * block:(b + 1) * block] * live_of(b)
        start[b] = piece
        window_a[b + halo] = piece.astype(BF16)

    pl.semaphore_wait(barrier, n_space - 1 + n_mode - 1)

    def halo_copies(window, base):
        to_right = pltpu.make_async_remote_copy(
            src_ref=window.at[pl.ds(slab_blocks, halo)], dst_ref=window.at[pl.ds(0, halo)],
            send_sem=halo_send.at[base], recv_sem=halo_recv.at[base],
            device_id={"space": right}, device_id_type=MESH)
        to_left = pltpu.make_async_remote_copy(
            src_ref=window.at[pl.ds(halo, halo)], dst_ref=window.at[pl.ds(slab_blocks + halo, halo)],
            send_sem=halo_send.at[base + 1], recv_sem=halo_recv.at[base + 1],
            device_id={"space": left}, device_id_type=MESH)
        return to_right, to_left

    halo_a = halo_copies(window_a, 0)
    halo_b = halo_copies(window_b, 2)
    for copy in halo_a:
        copy.start()
    for copy in halo_a:
        copy.wait_recv()

    def image_of(window, b):
        total = None
        for k in range(contacts):
            e = exponent_ref[b, k]
            scale = jnp.where(e > 0, F32(2.0), jnp.where(e < 0, F32(0.5), F32(1.0)))
            vec = window[column_ref[b, k]] * scale.astype(BF16)
            term = nt_dot(vec, hess[b, k])
            total = term if total is None else total + term
        return total

    def first_group(i, carry):
        c = lax.rem(i + groups - 1, groups)
        for half in range(GROUP):
            b = c * GROUP + half
            hess_copy(b).wait()
            piece = (image_of(window_a, b) - filter_center * start[b]) * (1.0 / filter_half) * live_of(b)
            first[b] = piece
            window_b[b + halo] = piece.astype(BF16)
        return carry

    lax.fori_loop(0, 2, first_group, 0)
    for copy in halo_b:
        copy.start()
    lax.fori_loop(2, groups, first_group, 0)

    def panel_copy(q, c):
        return pltpu.make_async_remote_copy(
            src_ref=panels_ref.at[q, c], dst_ref=panels_ref.at[q, c],
            send_sem=panel_send.at[q, c], recv_sem=panel_recv.at[q, c],
            device_id={"mode": above}, device_id_type=MESH)

    has_above = level < n_mode - 1
    gacc[...] = jnp.zeros_like(gacc)

    def second_group(i, carry):
        c = lax.rem(i + 1, groups)
        for half in range(GROUP):
            b = c * GROUP + half
            piece = (2.0 / filter_half * (image_of(window_b, b) - filter_center * first[b]) - start[b]) * live_of(b)
            own_ref[c, :, half * block:(half + 1) * block] = piece
        panels_ref[level, c] = own_ref[c].astype(BF16)

        @pl.when(has_above)
        def _():
            panel_copy(level, c).start()

        whole = own_ref[c]
        gacc[level] += nt_dot(whole, whole, HIGHEST)
        return carry

    for copy in halo_b:
        copy.wait_recv()
    lax.fori_loop(0, groups, second_group, 0)

    for d in range(1, n_mode):
        @pl.when(level >= d)
        def _():
            q = lax.rem(level - d + n_mode, n_mode)

            def arrival(i, carry):
                c = lax.rem(i + 1, groups)
                panel_copy(q, c).wait_recv()

                @pl.when(has_above)
                def _():
                    panel_copy(q, c).start()

                whole = own_ref[c]
                high = whole.astype(BF16)
                low = (whole - high.astype(F32)).astype(BF16)
                other = panels_ref[q, c]
                gacc[q] += nt_dot(high, other) + nt_dot(low, other)
                return carry

            lax.fori_loop(0, groups, arrival, 0)

    for q in range(n_mode):
        for s in range(n_space):
            gsend[s, :, q * panel_size:(q + 1) * panel_size] = gacc[q, s * share:(s + 1) * share, :]

    def rs_copy(target, slot):
        return pltpu.make_async_remote_copy(
            src_ref=gsend.at[target], dst_ref=grecv.at[slot],
            send_sem=rs_send.at[target], recv_sem=rs_recv.at[slot],
            device_id={"space": target}, device_id_type=MESH)

    for step in range(1, n_space):
        rs_copy(lax.rem(here + step, n_space), here).start()
    total = gsend[here]
    for step in range(1, n_space):
        peer = lax.rem(here + step, n_space)
        rs_copy(peer, peer).wait_recv()
        total = total + grecv[peer]
    gz[level] = total

    def z_copy(target, slot):
        return pltpu.make_async_remote_copy(
            src_ref=gz.at[slot], dst_ref=gz.at[slot],
            send_sem=z_send.at[target], recv_sem=z_recv.at[slot],
            device_id={"mode": target}, device_id_type=MESH)

    for step in range(1, n_mode):
        @pl.when(level + step < n_mode)
        def _():
            higher = lax.rem(level + step, n_mode)
            z_copy(higher, level).start()
            gz[higher] = jnp.zeros_like(total)

    for step in range(1, n_mode):
        @pl.when(level >= step)
        def _():
            lower = lax.rem(level - step + n_mode, n_mode)
            z_copy(lower, lower).wait_recv()

    def ag_copy(target, slot):
        return pltpu.make_async_remote_copy(
            src_ref=gz, dst_ref=gram_ref.at[slot],
            send_sem=ag_send.at[target], recv_sem=ag_recv.at[slot],
            device_id={"space": target}, device_id_type=MESH)

    for step in range(1, n_space):
        ag_copy(lax.rem(here + step, n_space), here).start()
    gram_ref[here] = gz[...]
    for step in range(1, n_space):
        peer = lax.rem(here + step, n_space)
        ag_copy(peer, peer).wait_recv()

    for copy in halo_a:
        copy.wait_send()
    for copy in halo_b:
        copy.wait_send()
    for step in range(1, n_space):
        peer = lax.rem(here + step, n_space)
        rs_copy(peer, here).wait_send()
        ag_copy(peer, here).wait_send()
    for step in range(1, n_mode):
        @pl.when(level + step < n_mode)
        def _():
            z_copy(lax.rem(level + step, n_mode), level).wait_send()
    for d in range(n_mode):
        @pl.when(has_above & (level >= d))
        def _():
            q = lax.rem(level - d + n_mode, n_mode)

            def sent(c, carry):
                panel_copy(q, c).wait_send()
                return carry

            lax.fori_loop(0, groups, sent, 0)


def finish_kernel(gram_ref, own_ref, panels_ref, out_ref, scaled, inverse, extra):
    n_mode, groups, panel_size, width = panels_ref.shape
    size = gram_ref.shape[0]
    level = lax.axis_index("mode")
    rows = lax.broadcasted_iota(jnp.int32, (size, size), 0)
    cols = lax.broadcasted_iota(jnp.int32, (size, size), 1)
    eye = (rows == cols).astype(F32)
    edge = (level + 1) * panel_size
    gram = jnp.where(rows < edge, gram_ref[...], eye)
    gram = jnp.where(rows >= cols, gram, 0.0)
    diag_col = jnp.sum(jnp.where(rows == cols, gram, 0.0), axis=1, keepdims=True)
    diag_row = jnp.sum(jnp.where(rows == cols, gram, 0.0), axis=0, keepdims=True)
    scale_col = lax.rsqrt(diag_col)
    scale_row = lax.rsqrt(diag_row)
    lower = jnp.where(rows > cols, gram * scale_col * scale_row, 0.0)
    scaled[...] = lower + lower.T + eye

    def half_lower(error):
        return jnp.where(rows > cols, error, jnp.where(rows == cols, 0.5 * error, 0.0))

    def dot(a, b):
        return jnp.dot(a, b, precision=HIGHEST, preferred_element_type=F32)

    inverse[...] = eye - lower

    def unfinished(state):
        step, worst = state
        return (worst > 1e-3) & (step < 12)

    def improve(state):
        step, _ = state
        x = inverse[...]
        error = nt_dot(dot(x, scaled[...]), x, HIGHEST) - eye
        worst = jnp.max(jnp.abs(error))
        inverse[...] = x - dot(half_lower(error), x)
        return step + 1, jnp.where(worst < 1e30, worst, F32(1e30))

    _, worst = lax.while_loop(unfinished, improve, (0, F32(1.0)))

    @pl.when(jnp.logical_not(worst <= 1e-3))
    def _():
        inverse[...] = eye
        extra[...] = scaled[...]

        def eliminate(j, carry):
            pivot_row = extra[pl.ds(j, 1), :]
            pivot = jnp.sum(jnp.where(lax.broadcasted_iota(jnp.int32, (1, size), 1) == j, pivot_row, 0.0), axis=1, keepdims=True)
            x_row = inverse[pl.ds(j, 1), :]
            column = jnp.sum(jnp.where(cols == j, extra[...], 0.0), axis=1, keepdims=True)
            index = lax.broadcasted_iota(jnp.int32, (size, 1), 0)
            factor = jnp.where(index > j, column / pivot, 0.0)
            extra[...] = extra[...] - factor * pivot_row
            inverse[...] = inverse[...] - factor * x_row
            return carry

        lax.fori_loop(0, size, eliminate, 0)
        pivots = jnp.sum(jnp.where(rows == cols, extra[...], 0.0), axis=1, keepdims=True)
        inverse[...] = inverse[...] * lax.rsqrt(pivots)

    inverse[...] = inverse[...] * scale_row
    mine = inverse[pl.ds(pl.multiple_of(level * panel_size, panel_size), panel_size), :]
    for q in range(n_mode):
        part = mine[:, q * panel_size:(q + 1) * panel_size]

        @pl.when(q == level)
        def _():
            extra[:panel_size, :panel_size] = part

    for c in range(groups):
        out_ref[:, c * width:(c + 1) * width] = dot(extra[:panel_size, :panel_size], own_ref[c])
    for q in range(n_mode - 1):
        @pl.when(q < level)
        def _():
            part = mine[:, q * panel_size:(q + 1) * panel_size].astype(BF16)
            for c in range(groups):
                out_ref[:, c * width:(c + 1) * width] += jnp.dot(part, panels_ref[q, c], preferred_element_type=F32)


def per_device(n_space, n_mode, start_modes, hessian, block_exponent, col_block, grain_count):
    panel_size, rows_here = start_modes.shape
    slab_blocks, contacts, block, _ = hessian.shape
    groups, width = slab_blocks // GROUP, GROUP * block
    share = panel_size // n_space
    modes = panel_size * n_mode
    window = slab_blocks + 2 * HALO_BLOCKS
    vmem = pl.BlockSpec(memory_space=pltpu.VMEM)
    smem = pl.BlockSpec(memory_space=pltpu.SMEM)
    dma = pltpu.SemaphoreType.DMA
    own, panels, gram = pl.pallas_call(
        functools.partial(filter_kernel, n_space, n_mode),
        out_shape=(
            jax.ShapeDtypeStruct((groups, panel_size, width), F32),
            jax.ShapeDtypeStruct((n_mode, groups, panel_size, width), BF16),
            jax.ShapeDtypeStruct((n_space, n_mode, share, modes), F32),
        ),
        in_specs=[smem, smem, smem, vmem, pl.BlockSpec(memory_space=pl.ANY)],
        out_specs=(vmem, vmem, vmem),
        scratch_shapes=[
            pltpu.VMEM(hessian.shape, BF16),
            pltpu.VMEM((slab_blocks, panel_size, block), F32),
            pltpu.VMEM((slab_blocks, panel_size, block), F32),
            pltpu.VMEM((window, panel_size, block), BF16),
            pltpu.VMEM((window, panel_size, block), BF16),
            pltpu.VMEM((n_mode, panel_size, panel_size), F32),
            pltpu.VMEM((n_space, share, modes), F32),
            pltpu.VMEM((n_space, share, modes), F32),
            pltpu.VMEM((n_mode, share, modes), F32),
            dma((slab_blocks,)), dma((4,)), dma((4,)),
            dma((n_mode, groups)), dma((n_mode, groups)),
            dma((n_space,)), dma((n_space,)), dma((n_mode,)), dma((n_mode,)),
            dma((n_space,)), dma((n_space,)),
        ],
        compiler_params=pltpu.CompilerParams(collective_id=0, has_side_effects=True),
        name="filter",
    )(block_exponent, col_block, grain_count, start_modes, hessian)
    gram = jnp.transpose(gram, (1, 0, 2, 3)).reshape(modes, modes)
    return pl.pallas_call(
        finish_kernel,
        out_shape=jax.ShapeDtypeStruct(start_modes.shape, F32),
        in_specs=[vmem, vmem, vmem],
        out_specs=vmem,
        scratch_shapes=[pltpu.VMEM((modes, modes), F32)] * 3,
        name="finish",
    )(gram, own, panels)


def solution(mesh):
    return jax.shard_map(
        functools.partial(per_device, mesh.shape["space"], mesh.shape["mode"]),
        mesh=mesh,
        in_specs=(
            P("mode", "space"),
            P("space", None, None, None),
            P("space", None),
            P("space", None),
            P("space"),
        ),
        out_specs=P("mode", "space"),
        check_vma=False,
    )
```

```python
import functools

import jax
import jax.numpy as jnp
from jax import lax
from jax.experimental import pallas as pl
from jax.experimental.pallas import tpu as pltpu
from jax.sharding import PartitionSpec as P

HALO_BLOCKS = 2
GROUP = 2

filter_center = -0.5
filter_half = 1.5

F32 = jnp.float32
BF16 = jnp.bfloat16
MESH = pl.DeviceIdType.MESH
HIGHEST = lax.Precision.HIGHEST


def nt_dot(a, b, precision=None):
    return lax.dot_general(
        a, b, (((1,), (1,)), ((), ())), precision=precision, preferred_element_type=F32
    )


def filter_kernel(
    n_space, n_mode, exponent_hbm, column_hbm, count_ref, start_ref, hessian_ref,
    own_ref, panels_ref, gram_ref,
    exponent_ref, column_ref, hess, start, first, window_a, window_b, gacc, gsend, grecv, gz,
    table_sem, hess_sem, halo_send, halo_recv, panel_send, panel_recv, rs_send, rs_recv,
    z_send, z_recv, ag_send, ag_recv, down_send, down_recv,
):
    panel_size = start_ref.shape[0]
    slab_blocks, contacts, block, _ = hessian_ref.shape
    groups = slab_blocks // GROUP
    halo = HALO_BLOCKS
    share = panel_size // n_space
    here = lax.axis_index("space")
    level = lax.axis_index("mode")
    right = lax.rem(here + 1, n_space)
    left = lax.rem(here + n_space - 1, n_space)
    above = lax.rem(level + 1, n_mode)

    def hess_copy(b):
        return pltpu.make_async_copy(hessian_ref.at[b], hess.at[b], hess_sem.at[b])

    tables = (
        pltpu.make_async_copy(exponent_hbm, exponent_ref, table_sem.at[0]),
        pltpu.make_async_copy(column_hbm, column_ref, table_sem.at[1]),
    )
    for copy in tables:
        copy.start()

    @pl.loop(0, slab_blocks)
    def _(i):
        hess_copy(lax.rem(i + slab_blocks - GROUP, slab_blocks)).start()

    barrier = pltpu.get_barrier_semaphore()
    for step in range(1, n_space):
        pl.semaphore_signal(barrier, inc=1, device_id={"space": lax.rem(here + step, n_space)}, device_id_type=MESH)
    for step in range(1, n_mode):
        pl.semaphore_signal(barrier, inc=1, device_id={"mode": lax.rem(level + step, n_mode)}, device_id_type=MESH)

    live_count = 6 * count_ref[0]

    def live_of(b):
        places = lax.broadcasted_iota(jnp.int32, (panel_size, block), 1) + b * block
        return (places < live_count).astype(F32)

    for b in range(slab_blocks):
        piece = start_ref[:, b * block:(b + 1) * block] * live_of(b)
        start[b] = piece
        window_a[b + halo] = piece.astype(BF16)

    for copy in tables:
        copy.wait()
    pl.semaphore_wait(barrier, n_space - 1 + n_mode - 1)

    def halo_copies(window, base):
        to_right = pltpu.make_async_remote_copy(
            src_ref=window.at[pl.ds(slab_blocks, halo)], dst_ref=window.at[pl.ds(0, halo)],
            send_sem=halo_send.at[base], recv_sem=halo_recv.at[base],
            device_id={"space": right}, device_id_type=MESH)
        to_left = pltpu.make_async_remote_copy(
            src_ref=window.at[pl.ds(halo, halo)], dst_ref=window.at[pl.ds(slab_blocks + halo, halo)],
            send_sem=halo_send.at[base + 1], recv_sem=halo_recv.at[base + 1],
            device_id={"space": left}, device_id_type=MESH)
        return to_right, to_left

    halo_a = halo_copies(window_a, 0)
    halo_b = halo_copies(window_b, 2)
    for copy in halo_a:
        copy.start()
    for copy in halo_a:
        copy.wait_recv()

    def image_of(window, b):
        total = None
        for k in range(contacts):
            e = exponent_ref[b, k]
            scale = jnp.where(e > 0, F32(2.0), jnp.where(e < 0, F32(0.5), F32(1.0)))
            vec = window[column_ref[b, k]] * scale.astype(BF16)
            term = nt_dot(vec, hess[b, k])
            total = term if total is None else total + term
        return total

    def first_group(i, carry):
        c = lax.rem(i + groups - 1, groups)
        for half in range(GROUP):
            b = c * GROUP + half
            hess_copy(b).wait()
            piece = (image_of(window_a, b) - filter_center * start[b]) * (1.0 / filter_half) * live_of(b)
            first[b] = piece
            window_b[b + halo] = piece.astype(BF16)
        return carry

    lax.fori_loop(0, 2, first_group, 0)
    for copy in halo_b:
        copy.start()
    lax.fori_loop(2, groups, first_group, 0)

    def panel_copy(q, c):
        return pltpu.make_async_remote_copy(
            src_ref=panels_ref.at[q, c], dst_ref=panels_ref.at[q, c],
            send_sem=panel_send.at[q, c], recv_sem=panel_recv.at[q, c],
            device_id={"mode": above}, device_id_type=MESH)

    has_above = level < n_mode - 1
    top = n_mode - 1
    early = n_mode >= 3
    below = lax.rem(level + n_mode - 1, n_mode)

    def down_copy(c):
        return pltpu.make_async_remote_copy(
            src_ref=panels_ref.at[top, c], dst_ref=panels_ref.at[top, c],
            send_sem=down_send.at[c], recv_sem=down_recv.at[c],
            device_id={"mode": below}, device_id_type=MESH)

    def split(x):
        high = x.astype(BF16)
        return high, (x - high.astype(F32)).astype(BF16)

    gacc[...] = jnp.zeros_like(gacc)

    def second_group(i, carry):
        c = lax.rem(i + 1, groups)
        for half in range(GROUP):
            b = c * GROUP + half
            piece = (2.0 / filter_half * (image_of(window_b, b) - filter_center * first[b]) - start[b]) * live_of(b)
            own_ref[c, :, half * block:(half + 1) * block] = piece
        panels_ref[level, c] = own_ref[c].astype(BF16)

        @pl.when(has_above)
        def _():
            panel_copy(level, c).start()

        if early:
            @pl.when(level == top)
            def _():
                down_copy(c).start()

        high, low = split(own_ref[c])
        gacc[level] += nt_dot(high, high) + (nt_dot(high, low) + nt_dot(low, high))
        return carry

    for copy in halo_b:
        copy.wait_recv()
    lax.fori_loop(0, groups, second_group, 0)

    for d in range(1, n_mode):
        late = early and d == top

        @pl.when(level >= d)
        def _():
            q = lax.rem(level - d + n_mode, n_mode)

            def arrival(i, carry):
                c = lax.rem(i + 1, groups)
                panel_copy(q, c).wait_recv()

                @pl.when(has_above)
                def _():
                    panel_copy(q, c).start()

                high, low = split(own_ref[c])
                other = panels_ref[q, c]
                gacc[q] += nt_dot(high, other) + nt_dot(low, other)
                return carry

            if not late:
                lax.fori_loop(0, groups, arrival, 0)

    if early:
        @pl.when(level == top - 1)
        def _():
            def meeting(i, carry):
                c = lax.rem(i + 1, groups)
                down_copy(c).wait_recv()
                gacc[n_mode] += nt_dot(panels_ref[top, c], panels_ref[0, c])
                return carry

            lax.fori_loop(0, groups, meeting, 0)

    for q in range(n_mode + 1):
        for s in range(n_space):
            gsend[s, :, q * panel_size:(q + 1) * panel_size] = gacc[q, s * share:(s + 1) * share, :]

    def rs_copy(target, slot):
        return pltpu.make_async_remote_copy(
            src_ref=gsend.at[target], dst_ref=grecv.at[slot],
            send_sem=rs_send.at[target], recv_sem=rs_recv.at[slot],
            device_id={"space": target}, device_id_type=MESH)

    for step in range(1, n_space):
        rs_copy(lax.rem(here + step, n_space), here).start()
    total = gsend[here]
    for step in range(1, n_space):
        peer = lax.rem(here + step, n_space)
        rs_copy(peer, peer).wait_recv()
        total = total + grecv[peer]
    gz[level] = total

    def z_copy(target, slot):
        return pltpu.make_async_remote_copy(
            src_ref=gz.at[slot], dst_ref=gz.at[slot],
            send_sem=z_send.at[target], recv_sem=z_recv.at[slot],
            device_id={"mode": target}, device_id_type=MESH)

    for step in range(1, n_mode):
        @pl.when(level + step < n_mode)
        def _():
            higher = lax.rem(level + step, n_mode)
            z_copy(higher, level).start()
            gz[higher] = jnp.zeros_like(total)

    for step in range(1, n_mode):
        @pl.when(level >= step)
        def _():
            lower = lax.rem(level - step + n_mode, n_mode)
            z_copy(lower, lower).wait_recv()

    if early:
        @pl.when(level == top)
        def _():
            met = gz[top - 1, :, n_mode * panel_size:]
            gz[top, :, :panel_size] = gz[top, :, :panel_size] + met

    def ag_copy(target, slot):
        return pltpu.make_async_remote_copy(
            src_ref=gz, dst_ref=gram_ref.at[slot],
            send_sem=ag_send.at[target], recv_sem=ag_recv.at[slot],
            device_id={"space": target}, device_id_type=MESH)

    for step in range(1, n_space):
        ag_copy(lax.rem(here + step, n_space), here).start()
    gram_ref[here] = gz[...]
    for step in range(1, n_space):
        peer = lax.rem(here + step, n_space)
        ag_copy(peer, peer).wait_recv()

    if early:
        @pl.when(level == top)
        def _():
            def landed(i, carry):
                c = lax.rem(i + 1, groups)
                panel_copy(0, c).wait_recv()
                down_copy(c).wait_send()
                return carry

            lax.fori_loop(0, groups, landed, 0)

    for copy in halo_a:
        copy.wait_send()
    for copy in halo_b:
        copy.wait_send()
    for step in range(1, n_space):
        peer = lax.rem(here + step, n_space)
        rs_copy(peer, here).wait_send()
        ag_copy(peer, here).wait_send()
    for step in range(1, n_mode):
        @pl.when(level + step < n_mode)
        def _():
            z_copy(lax.rem(level + step, n_mode), level).wait_send()
    for d in range(n_mode):
        @pl.when(has_above & (level >= d))
        def _():
            q = lax.rem(level - d + n_mode, n_mode)

            def sent(c, carry):
                panel_copy(q, c).wait_send()
                return carry

            lax.fori_loop(0, groups, sent, 0)


def finish_kernel(gram_ref, own_ref, panels_ref, out_ref, scaled, inverse, extra):
    n_mode, groups, panel_size, width = panels_ref.shape
    n_space, _, share, _ = gram_ref.shape
    size = n_mode * panel_size
    for q in range(n_mode):
        for s in range(n_space):
            base = q * panel_size + s * share
            extra[base:base + share, :] = gram_ref[s, q, :, :size]
    level = lax.axis_index("mode")
    rows = lax.broadcasted_iota(jnp.int32, (size, size), 0)
    cols = lax.broadcasted_iota(jnp.int32, (size, size), 1)
    eye = (rows == cols).astype(F32)
    edge = (level + 1) * panel_size
    gram = jnp.where(rows < edge, extra[...], eye)
    gram = jnp.where(rows >= cols, gram, 0.0)
    diag_col = jnp.sum(jnp.where(rows == cols, gram, 0.0), axis=1, keepdims=True)
    diag_row = jnp.sum(jnp.where(rows == cols, gram, 0.0), axis=0, keepdims=True)
    scale_col = lax.rsqrt(diag_col)
    scale_row = lax.rsqrt(diag_row)
    lower = jnp.where(rows > cols, gram * scale_col * scale_row, 0.0)
    scaled[...] = lower + lower.T + eye

    def half_lower(error):
        return jnp.where(rows > cols, error, jnp.where(rows == cols, 0.5 * error, 0.0))

    def dot(a, b):
        return jnp.dot(a, b, precision=HIGHEST, preferred_element_type=F32)

    x = eye - lower
    low_scaled = scaled[...].astype(BF16)
    for _ in range(2):
        low_x = x.astype(BF16)
        moved = jnp.dot(low_x, low_scaled, preferred_element_type=F32)
        error = nt_dot(moved.astype(BF16), low_x) - eye
        x = x - jnp.dot(half_lower(error).astype(BF16), low_x, preferred_element_type=F32)
    inverse[...] = x

    def unfinished(state):
        step, worst = state
        return (worst > 1e-3) & (step < 12)

    def improve(state):
        step, _ = state
        x = inverse[...]
        error = nt_dot(dot(x, scaled[...]), x, HIGHEST) - eye
        worst = jnp.max(jnp.abs(error))
        inverse[...] = x - dot(half_lower(error), x)
        return step + 1, jnp.where(worst < 1e30, worst, F32(1e30))

    _, worst = lax.while_loop(unfinished, improve, (0, F32(1.0)))

    @pl.when(jnp.logical_not(worst <= 1e-3))
    def _():
        inverse[...] = eye
        extra[...] = scaled[...]

        def eliminate(j, carry):
            pivot_row = extra[pl.ds(j, 1), :]
            pivot = jnp.sum(jnp.where(lax.broadcasted_iota(jnp.int32, (1, size), 1) == j, pivot_row, 0.0), axis=1, keepdims=True)
            x_row = inverse[pl.ds(j, 1), :]
            column = jnp.sum(jnp.where(cols == j, extra[...], 0.0), axis=1, keepdims=True)
            index = lax.broadcasted_iota(jnp.int32, (size, 1), 0)
            factor = jnp.where(index > j, column / pivot, 0.0)
            extra[...] = extra[...] - factor * pivot_row
            inverse[...] = inverse[...] - factor * x_row
            return carry

        lax.fori_loop(0, size, eliminate, 0)
        pivots = jnp.sum(jnp.where(rows == cols, extra[...], 0.0), axis=1, keepdims=True)
        inverse[...] = inverse[...] * lax.rsqrt(pivots)

    inverse[...] = inverse[...] * scale_row
    mine = inverse[pl.ds(pl.multiple_of(level * panel_size, panel_size), panel_size), :]
    for q in range(n_mode):
        part = mine[:, q * panel_size:(q + 1) * panel_size]

        @pl.when(q == level)
        def _():
            extra[:panel_size, :panel_size] = part

    for c in range(groups):
        out_ref[:, c * width:(c + 1) * width] = dot(extra[:panel_size, :panel_size], own_ref[c])
    for q in range(n_mode - 1):
        @pl.when(q < level)
        def _():
            part = mine[:, q * panel_size:(q + 1) * panel_size].astype(BF16)
            for c in range(groups):
                out_ref[:, c * width:(c + 1) * width] += jnp.dot(part, panels_ref[q, c], preferred_element_type=F32)


def per_device(n_space, n_mode, start_modes, hessian, block_exponent, col_block, grain_count):
    panel_size, rows_here = start_modes.shape
    slab_blocks, contacts, block, _ = hessian.shape
    groups, width = slab_blocks // GROUP, GROUP * block
    share = panel_size // n_space
    modes = panel_size * n_mode
    window = slab_blocks + 2 * HALO_BLOCKS
    vmem = pl.BlockSpec(memory_space=pltpu.VMEM)
    smem = pl.BlockSpec(memory_space=pltpu.SMEM)
    hbm = pl.BlockSpec(memory_space=pl.ANY)
    dma = pltpu.SemaphoreType.DMA
    own, panels, gram = pl.pallas_call(
        functools.partial(filter_kernel, n_space, n_mode),
        out_shape=(
            jax.ShapeDtypeStruct((groups, panel_size, width), F32),
            jax.ShapeDtypeStruct((n_mode, groups, panel_size, width), BF16),
            jax.ShapeDtypeStruct((n_space, n_mode, share, modes + panel_size), F32),
        ),
        in_specs=[hbm, hbm, smem, vmem, hbm],
        out_specs=(vmem, vmem, vmem),
        scratch_shapes=[
            pltpu.SMEM(block_exponent.shape, jnp.int32),
            pltpu.SMEM(col_block.shape, jnp.int32),
            pltpu.VMEM(hessian.shape, BF16),
            pltpu.VMEM((slab_blocks, panel_size, block), F32),
            pltpu.VMEM((slab_blocks, panel_size, block), F32),
            pltpu.VMEM((window, panel_size, block), BF16),
            pltpu.VMEM((window, panel_size, block), BF16),
            pltpu.VMEM((n_mode + 1, panel_size, panel_size), F32),
            pltpu.VMEM((n_space, share, modes + panel_size), F32),
            pltpu.VMEM((n_space, share, modes + panel_size), F32),
            pltpu.VMEM((n_mode, share, modes + panel_size), F32),
            dma((2,)), dma((slab_blocks,)), dma((4,)), dma((4,)),
            dma((n_mode, groups)), dma((n_mode, groups)),
            dma((n_space,)), dma((n_space,)), dma((n_mode,)), dma((n_mode,)),
            dma((n_space,)), dma((n_space,)), dma((groups,)), dma((groups,)),
        ],
        compiler_params=pltpu.CompilerParams(collective_id=0, has_side_effects=True),
        name="filter",
    )(block_exponent, col_block, grain_count, start_modes, hessian)
    return pl.pallas_call(
        finish_kernel,
        out_shape=jax.ShapeDtypeStruct(start_modes.shape, F32),
        in_specs=[vmem, vmem, vmem],
        out_specs=vmem,
        scratch_shapes=[pltpu.VMEM((modes, modes), F32)] * 3,
        name="finish",
    )(gram, own, panels)


def solution(mesh):
    return jax.shard_map(
        functools.partial(per_device, mesh.shape["space"], mesh.shape["mode"]),
        mesh=mesh,
        in_specs=(
            P("mode", "space"),
            P("space", None, None, None),
            P("space", None),
            P("space", None),
            P("space"),
        ),
        out_specs=P("mode", "space"),
        check_vma=False,
    )
```

```python
import functools

import jax
import jax.numpy as jnp
from jax import lax
from jax.experimental import pallas as pl
from jax.experimental.pallas import tpu as pltpu
from jax.sharding import PartitionSpec as P

HALO_BLOCKS = 2
GROUP = 2

filter_center = -0.5
filter_half = 1.5

F32 = jnp.float32
BF16 = jnp.bfloat16
MESH = pl.DeviceIdType.MESH
HIGHEST = lax.Precision.HIGHEST


def nt_dot(a, b, precision=None):
    return lax.dot_general(
        a, b, (((1,), (1,)), ((), ())), precision=precision, preferred_element_type=F32
    )


def filter_kernel(
    n_space, n_mode, exponent_hbm, column_hbm, count_ref, start_ref, hessian_ref,
    own_ref, panels_ref, gram_ref,
    exponent_ref, column_ref, hess, start, first, window_a, window_b, gacc, gsend, grecv, gz,
    table_sem, hess_sem, halo_send, halo_recv, panel_send, panel_recv, rs_send, rs_recv,
    z_send, z_recv, ag_send, ag_recv, down_send, down_recv,
):
    panel_size = start_ref.shape[0]
    slab_blocks, contacts, block, _ = hessian_ref.shape
    groups = slab_blocks // GROUP
    halo = HALO_BLOCKS
    share = panel_size // n_space
    here = lax.axis_index("space")
    level = lax.axis_index("mode")
    right = lax.rem(here + 1, n_space)
    left = lax.rem(here + n_space - 1, n_space)
    above = lax.rem(level + 1, n_mode)

    def hess_copy(b):
        return pltpu.make_async_copy(hessian_ref.at[b], hess.at[b], hess_sem.at[b])

    tables = (
        pltpu.make_async_copy(exponent_hbm, exponent_ref, table_sem.at[0]),
        pltpu.make_async_copy(column_hbm, column_ref, table_sem.at[1]),
    )
    for copy in tables:
        copy.start()

    @pl.loop(0, slab_blocks)
    def _(i):
        hess_copy(lax.rem(i + slab_blocks - GROUP, slab_blocks)).start()

    barrier = pltpu.get_barrier_semaphore()
    for step in range(1, n_space):
        pl.semaphore_signal(barrier, inc=1, device_id={"space": lax.rem(here + step, n_space)}, device_id_type=MESH)
    for step in range(1, n_mode):
        pl.semaphore_signal(barrier, inc=1, device_id={"mode": lax.rem(level + step, n_mode)}, device_id_type=MESH)

    live_count = 6 * count_ref[0]

    def live_of(b):
        places = lax.broadcasted_iota(jnp.int32, (panel_size, block), 1) + b * block
        return (places < live_count).astype(F32)

    for b in range(slab_blocks):
        piece = start_ref[:, b * block:(b + 1) * block] * live_of(b)
        start[b] = piece
        window_a[b + halo] = piece.astype(BF16)

    for copy in tables:
        copy.wait()
    pl.semaphore_wait(barrier, n_space - 1 + n_mode - 1)

    def halo_copies(window, base):
        to_right = pltpu.make_async_remote_copy(
            src_ref=window.at[pl.ds(slab_blocks, halo)], dst_ref=window.at[pl.ds(0, halo)],
            send_sem=halo_send.at[base], recv_sem=halo_recv.at[base],
            device_id={"space": right}, device_id_type=MESH)
        to_left = pltpu.make_async_remote_copy(
            src_ref=window.at[pl.ds(halo, halo)], dst_ref=window.at[pl.ds(slab_blocks + halo, halo)],
            send_sem=halo_send.at[base + 1], recv_sem=halo_recv.at[base + 1],
            device_id={"space": left}, device_id_type=MESH)
        return to_right, to_left

    halo_a = halo_copies(window_a, 0)
    halo_b = halo_copies(window_b, 2)
    for copy in halo_a:
        copy.start()
    for copy in halo_a:
        copy.wait_recv()

    def image_of(window, b):
        total = None
        for k in range(contacts):
            e = exponent_ref[k, b]
            scale = jnp.where(e > 0, F32(2.0), jnp.where(e < 0, F32(0.5), F32(1.0)))
            vec = window[column_ref[k, b]] * scale.astype(BF16)
            term = nt_dot(vec, hess[b, k])
            total = term if total is None else total + term
        return total

    def first_group(i, carry):
        c = lax.rem(i + groups - 1, groups)
        for half in range(GROUP):
            b = c * GROUP + half
            hess_copy(b).wait()
            piece = (image_of(window_a, b) - filter_center * start[b]) * (1.0 / filter_half) * live_of(b)
            first[b] = piece
            window_b[b + halo] = piece.astype(BF16)
        return carry

    lax.fori_loop(0, 2, first_group, 0)
    for copy in halo_b:
        copy.start()
    lax.fori_loop(2, groups, first_group, 0)

    def panel_copy(q, c):
        return pltpu.make_async_remote_copy(
            src_ref=panels_ref.at[q, c], dst_ref=panels_ref.at[q, c],
            send_sem=panel_send.at[q, c], recv_sem=panel_recv.at[q, c],
            device_id={"mode": above}, device_id_type=MESH)

    has_above = level < n_mode - 1
    top = n_mode - 1
    early = n_mode >= 3
    below = lax.rem(level + n_mode - 1, n_mode)

    def down_copy(c):
        return pltpu.make_async_remote_copy(
            src_ref=panels_ref.at[top, c], dst_ref=panels_ref.at[top, c],
            send_sem=down_send.at[c], recv_sem=down_recv.at[c],
            device_id={"mode": below}, device_id_type=MESH)

    def split(x):
        high = x.astype(BF16)
        return high, (x - high.astype(F32)).astype(BF16)

    gacc[...] = jnp.zeros_like(gacc)

    def second_group(i, carry):
        c = lax.rem(i + 1, groups)
        for half in range(GROUP):
            b = c * GROUP + half
            piece = (2.0 / filter_half * (image_of(window_b, b) - filter_center * first[b]) - start[b]) * live_of(b)
            own_ref[c, :, half * block:(half + 1) * block] = piece
        panels_ref[level, c] = own_ref[c].astype(BF16)

        @pl.when(has_above)
        def _():
            panel_copy(level, c).start()

        if early:
            @pl.when(level == top)
            def _():
                down_copy(c).start()

        high, low = split(own_ref[c])
        gacc[level] += nt_dot(high, high) + (nt_dot(high, low) + nt_dot(low, high))
        return carry

    for copy in halo_b:
        copy.wait_recv()
    lax.fori_loop(0, groups, second_group, 0)

    for d in range(1, n_mode):
        late = early and d == top

        @pl.when(level >= d)
        def _():
            q = lax.rem(level - d + n_mode, n_mode)

            def arrival(i, carry):
                c = lax.rem(i + 1, groups)
                panel_copy(q, c).wait_recv()

                @pl.when(has_above)
                def _():
                    panel_copy(q, c).start()

                high, low = split(own_ref[c])
                other = panels_ref[q, c]
                gacc[q] += nt_dot(high, other) + nt_dot(low, other)
                if early and d == top - 1:
                    @pl.when(level == top - 1)
                    def _():
                        down_copy(c).wait_recv()
                        gacc[n_mode] += nt_dot(panels_ref[top, c], other)
                return carry

            if not late:
                lax.fori_loop(0, groups, arrival, 0)

    for q in range(n_mode + 1):
        for s in range(n_space):
            gsend[s, :, q * panel_size:(q + 1) * panel_size] = gacc[q, s * share:(s + 1) * share, :]

    def rs_copy(target, slot):
        return pltpu.make_async_remote_copy(
            src_ref=gsend.at[target], dst_ref=grecv.at[slot],
            send_sem=rs_send.at[target], recv_sem=rs_recv.at[slot],
            device_id={"space": target}, device_id_type=MESH)

    for step in range(1, n_space):
        rs_copy(lax.rem(here + step, n_space), here).start()
    total = gsend[here]
    for step in range(1, n_space):
        peer = lax.rem(here + step, n_space)
        rs_copy(peer, peer).wait_recv()
        total = total + grecv[peer]
    gz[level] = total

    def z_copy(target, slot):
        return pltpu.make_async_remote_copy(
            src_ref=gz.at[slot], dst_ref=gz.at[slot],
            send_sem=z_send.at[target], recv_sem=z_recv.at[slot],
            device_id={"mode": target}, device_id_type=MESH)

    for step in range(1, n_mode):
        @pl.when(level + step < n_mode)
        def _():
            z_copy(lax.rem(level + step, n_mode), level).start()

    def ag_copy(target, origin, slot):
        return pltpu.make_async_remote_copy(
            src_ref=gz.at[slot], dst_ref=gram_ref.at[origin, slot],
            send_sem=ag_send.at[target, slot], recv_sem=ag_recv.at[origin, slot],
            device_id={"space": target}, device_id_type=MESH)

    def spread(slot):
        for step in range(1, n_space):
            ag_copy(lax.rem(here + step, n_space), here, slot).start()
        gram_ref[here, slot] = gz[slot]

    spread(level)
    for q in range(n_mode - 1):
        @pl.when(q < level)
        def _():
            z_copy(q, q).wait_recv()
            spread(q)

    for q in range(n_mode):
        @pl.when(q <= level)
        def _():
            for step in range(1, n_space):
                peer = lax.rem(here + step, n_space)
                ag_copy(peer, peer, q).wait_recv()
                ag_copy(peer, here, q).wait_send()

    if early:
        @pl.when(level == top)
        def _():
            def landed(i, carry):
                c = lax.rem(i + 1, groups)
                panel_copy(0, c).wait_recv()
                down_copy(c).wait_send()
                return carry

            lax.fori_loop(0, groups, landed, 0)

    for copy in halo_a:
        copy.wait_send()
    for copy in halo_b:
        copy.wait_send()
    for step in range(1, n_space):
        peer = lax.rem(here + step, n_space)
        rs_copy(peer, here).wait_send()
    for step in range(1, n_mode):
        @pl.when(level + step < n_mode)
        def _():
            z_copy(lax.rem(level + step, n_mode), level).wait_send()
    for d in range(n_mode):
        @pl.when(has_above & (level >= d))
        def _():
            q = lax.rem(level - d + n_mode, n_mode)

            def sent(c, carry):
                panel_copy(q, c).wait_send()
                return carry

            lax.fori_loop(0, groups, sent, 0)


def finish_kernel(gram_ref, own_ref, panels_ref, out_ref, scaled, inverse, extra):
    n_mode, groups, panel_size, width = panels_ref.shape
    n_space, _, share, _ = gram_ref.shape
    size = n_mode * panel_size
    level = lax.axis_index("mode")
    for q in range(n_mode):
        for s in range(n_space):
            base = q * panel_size + s * share
            extra[base:base + share, :] = gram_ref[s, q, :, :size]

    if n_mode >= 3:
        @pl.when(level == n_mode - 1)
        def _():
            for s in range(n_space):
                base = size - panel_size + s * share
                extra[base:base + share, :panel_size] += gram_ref[s, n_mode - 2, :, size:]

    rows = lax.broadcasted_iota(jnp.int32, (size, size), 0)
    cols = lax.broadcasted_iota(jnp.int32, (size, size), 1)
    eye = (rows == cols).astype(F32)
    edge = (level + 1) * panel_size
    gram = jnp.where(rows < edge, extra[...], eye)
    gram = jnp.where(rows >= cols, gram, 0.0)
    diag_col = jnp.sum(jnp.where(rows == cols, gram, 0.0), axis=1, keepdims=True)
    diag_row = jnp.sum(jnp.where(rows == cols, gram, 0.0), axis=0, keepdims=True)
    scale_col = lax.rsqrt(diag_col)
    scale_row = lax.rsqrt(diag_row)
    lower = jnp.where(rows > cols, gram * scale_col * scale_row, 0.0)
    scaled[...] = lower + lower.T + eye

    def half_lower(error):
        return jnp.where(rows > cols, error, jnp.where(rows == cols, 0.5 * error, 0.0))

    def dot(a, b):
        return jnp.dot(a, b, precision=HIGHEST, preferred_element_type=F32)

    x = eye - lower
    low_scaled = scaled[...].astype(BF16)
    for _ in range(2):
        low_x = x.astype(BF16)
        moved = jnp.dot(low_x, low_scaled, preferred_element_type=F32)
        error = nt_dot(moved.astype(BF16), low_x) - eye
        x = x - jnp.dot(half_lower(error).astype(BF16), low_x, preferred_element_type=F32)
    inverse[...] = x

    def split(a):
        high = a.astype(BF16)
        return high, (a - high.astype(F32)).astype(BF16)

    def dot3(a, b, product=functools.partial(jnp.dot, preferred_element_type=F32)):
        return product(a[0], b[0]) + (product(a[0], b[1]) + product(a[1], b[0]))

    def unfinished(state):
        step, worst = state
        return (worst > 1e-3) & (step < 12)

    def improve(state):
        step, _ = state
        x = inverse[...]
        parts = split(x)
        error = dot3(split(dot3(parts, split(scaled[...]))), parts, nt_dot) - eye
        worst = jnp.max(jnp.abs(error))
        inverse[...] = x - dot3(split(half_lower(error)), parts)
        return step + 1, jnp.where(worst < 1e30, worst, F32(1e30))

    _, worst = lax.while_loop(unfinished, improve, (0, F32(1.0)))

    @pl.when(jnp.logical_not(worst <= 1e-3))
    def _():
        inverse[...] = eye
        extra[...] = scaled[...]

        def eliminate(j, carry):
            pivot_row = extra[pl.ds(j, 1), :]
            pivot = jnp.sum(jnp.where(lax.broadcasted_iota(jnp.int32, (1, size), 1) == j, pivot_row, 0.0), axis=1, keepdims=True)
            x_row = inverse[pl.ds(j, 1), :]
            column = jnp.sum(jnp.where(cols == j, extra[...], 0.0), axis=1, keepdims=True)
            index = lax.broadcasted_iota(jnp.int32, (size, 1), 0)
            factor = jnp.where(index > j, column / pivot, 0.0)
            extra[...] = extra[...] - factor * pivot_row
            inverse[...] = inverse[...] - factor * x_row
            return carry

        lax.fori_loop(0, size, eliminate, 0)
        pivots = jnp.sum(jnp.where(rows == cols, extra[...], 0.0), axis=1, keepdims=True)
        inverse[...] = inverse[...] * lax.rsqrt(pivots)

    inverse[...] = inverse[...] * scale_row
    mine = inverse[pl.ds(pl.multiple_of(level * panel_size, panel_size), panel_size), :]
    for q in range(n_mode):
        part = mine[:, q * panel_size:(q + 1) * panel_size]

        @pl.when(q == level)
        def _():
            extra[:panel_size, :panel_size] = part

    for c in range(groups):
        out_ref[:, c * width:(c + 1) * width] = dot(extra[:panel_size, :panel_size], own_ref[c])
    for q in range(n_mode - 1):
        @pl.when(q < level)
        def _():
            part = mine[:, q * panel_size:(q + 1) * panel_size].astype(BF16)
            for c in range(groups):
                out_ref[:, c * width:(c + 1) * width] += jnp.dot(part, panels_ref[q, c], preferred_element_type=F32)


def per_device(n_space, n_mode, start_modes, hessian, block_exponent, col_block, grain_count):
    panel_size, rows_here = start_modes.shape
    slab_blocks, contacts, block, _ = hessian.shape
    groups, width = slab_blocks // GROUP, GROUP * block
    share = panel_size // n_space
    modes = panel_size * n_mode
    window = slab_blocks + 2 * HALO_BLOCKS
    vmem = pl.BlockSpec(memory_space=pltpu.VMEM)
    smem = pl.BlockSpec(memory_space=pltpu.SMEM)
    hbm = pl.BlockSpec(memory_space=pl.ANY)
    dma = pltpu.SemaphoreType.DMA
    own, panels, gram = pl.pallas_call(
        functools.partial(filter_kernel, n_space, n_mode),
        out_shape=(
            jax.ShapeDtypeStruct((groups, panel_size, width), F32),
            jax.ShapeDtypeStruct((n_mode, groups, panel_size, width), BF16),
            jax.ShapeDtypeStruct((n_space, n_mode, share, modes + panel_size), F32),
        ),
        in_specs=[hbm, hbm, smem, vmem, hbm],
        out_specs=(vmem, vmem, vmem),
        scratch_shapes=[
            pltpu.SMEM((contacts, slab_blocks), jnp.int32),
            pltpu.SMEM((contacts, slab_blocks), jnp.int32),
            pltpu.VMEM(hessian.shape, BF16),
            pltpu.VMEM((slab_blocks, panel_size, block), F32),
            pltpu.VMEM((slab_blocks, panel_size, block), F32),
            pltpu.VMEM((window, panel_size, block), BF16),
            pltpu.VMEM((window, panel_size, block), BF16),
            pltpu.VMEM((n_mode + 1, panel_size, panel_size), F32),
            pltpu.VMEM((n_space, share, modes + panel_size), F32),
            pltpu.VMEM((n_space, share, modes + panel_size), F32),
            pltpu.VMEM((n_mode, share, modes + panel_size), F32),
            dma((2,)), dma((slab_blocks,)), dma((4,)), dma((4,)),
            dma((n_mode, groups)), dma((n_mode, groups)),
            dma((n_space,)), dma((n_space,)), dma((n_mode,)), dma((n_mode,)),
            dma((n_space, n_mode)), dma((n_space, n_mode)), dma((groups,)), dma((groups,)),
        ],
        compiler_params=pltpu.CompilerParams(collective_id=0, has_side_effects=True),
        name="filter",
    )(block_exponent.T, col_block.T, grain_count, start_modes, hessian)
    return pl.pallas_call(
        finish_kernel,
        out_shape=jax.ShapeDtypeStruct(start_modes.shape, F32),
        in_specs=[vmem, vmem, vmem],
        out_specs=vmem,
        scratch_shapes=[pltpu.VMEM((modes, modes), F32)] * 3,
        name="finish",
    )(gram, own, panels)


def solution(mesh):
    return jax.shard_map(
        functools.partial(per_device, mesh.shape["space"], mesh.shape["mode"]),
        mesh=mesh,
        in_specs=(
            P("mode", "space"),
            P("space", None, None, None),
            P("space", None),
            P("space", None),
            P("space"),
        ),
        out_specs=P("mode", "space"),
        check_vma=False,
    )
```

```python
import functools

import jax
import jax.numpy as jnp
from jax import lax
from jax.experimental import pallas as pl
from jax.experimental.pallas import tpu as pltpu
from jax.sharding import PartitionSpec as P

HALO_BLOCKS = 2
GROUP = 2

filter_center = -0.5
filter_half = 1.5

F32 = jnp.float32
BF16 = jnp.bfloat16
MESH = pl.DeviceIdType.MESH
HIGHEST = lax.Precision.HIGHEST


def nt_dot(a, b, precision=None):
    return lax.dot_general(
        a, b, (((1,), (1,)), ((), ())), precision=precision, preferred_element_type=F32
    )


def filter_kernel(
    n_space, n_mode, exponent_hbm, column_hbm, count_ref, start_ref, hessian_ref,
    own_ref, panels_ref, gram_ref,
    exponent_ref, column_ref, hess, start, first, window_a, window_b, gacc, gsend, grecv, gz,
    table_sem, hess_sem, halo_send, halo_recv, panel_send, panel_recv, rs_send, rs_recv,
    z_send, z_recv, ag_send, ag_recv, down_send, down_recv,
):
    panel_size = start_ref.shape[0]
    slab_blocks, contacts, block, _ = hessian_ref.shape
    groups = slab_blocks // GROUP
    halo = HALO_BLOCKS
    share = panel_size // n_space
    here = lax.axis_index("space")
    level = lax.axis_index("mode")
    right = lax.rem(here + 1, n_space)
    left = lax.rem(here + n_space - 1, n_space)
    above = lax.rem(level + 1, n_mode)

    def hess_copy(b):
        return pltpu.make_async_copy(hessian_ref.at[b], hess.at[b], hess_sem.at[b])

    tables = (
        pltpu.make_async_copy(exponent_hbm, exponent_ref, table_sem.at[0]),
        pltpu.make_async_copy(column_hbm, column_ref, table_sem.at[1]),
    )
    for copy in tables:
        copy.start()

    @pl.loop(0, slab_blocks)
    def _(i):
        hess_copy(lax.rem(i + slab_blocks - GROUP, slab_blocks)).start()

    barrier = pltpu.get_barrier_semaphore()
    for step in range(1, n_space):
        pl.semaphore_signal(barrier, inc=1, device_id={"space": lax.rem(here + step, n_space)}, device_id_type=MESH)
    for step in range(1, n_mode):
        pl.semaphore_signal(barrier, inc=1, device_id={"mode": lax.rem(level + step, n_mode)}, device_id_type=MESH)

    live_count = 6 * count_ref[0]

    def live_of(b):
        places = lax.broadcasted_iota(jnp.int32, (panel_size, block), 1) + b * block
        return (places < live_count).astype(F32)

    for b in range(slab_blocks):
        piece = start_ref[:, b * block:(b + 1) * block] * live_of(b)
        start[b] = piece
        window_a[b + halo] = piece.astype(BF16)

    for copy in tables:
        copy.wait()
    pl.semaphore_wait(barrier, n_space - 1 + n_mode - 1)

    def halo_copies(window, base):
        to_right = pltpu.make_async_remote_copy(
            src_ref=window.at[pl.ds(slab_blocks, halo)], dst_ref=window.at[pl.ds(0, halo)],
            send_sem=halo_send.at[base], recv_sem=halo_recv.at[base],
            device_id={"space": right}, device_id_type=MESH)
        to_left = pltpu.make_async_remote_copy(
            src_ref=window.at[pl.ds(halo, halo)], dst_ref=window.at[pl.ds(slab_blocks + halo, halo)],
            send_sem=halo_send.at[base + 1], recv_sem=halo_recv.at[base + 1],
            device_id={"space": left}, device_id_type=MESH)
        return to_right, to_left

    halo_a = halo_copies(window_a, 0)
    halo_b = halo_copies(window_b, 2)
    for copy in halo_a:
        copy.start()
    for copy in halo_a:
        copy.wait_recv()

    def image_of(window, b):
        total = None
        for k in range(contacts):
            e = exponent_ref[k, b]
            scale = jnp.where(e > 0, F32(2.0), jnp.where(e < 0, F32(0.5), F32(1.0)))
            vec = window[column_ref[k, b]] * scale.astype(BF16)
            term = nt_dot(vec, hess[b, k])
            total = term if total is None else total + term
        return total

    def first_group(i, carry):
        c = lax.rem(i + groups - 1, groups)
        for half in range(GROUP):
            b = c * GROUP + half
            hess_copy(b).wait()
            piece = (image_of(window_a, b) - filter_center * start[b]) * (1.0 / filter_half) * live_of(b)
            first[b] = piece
            window_b[b + halo] = piece.astype(BF16)
        return carry

    lax.fori_loop(0, 2, first_group, 0)
    for copy in halo_b:
        copy.start()
    lax.fori_loop(2, groups, first_group, 0)

    def panel_copy(q, c):
        return pltpu.make_async_remote_copy(
            src_ref=panels_ref.at[q, c], dst_ref=panels_ref.at[q, c],
            send_sem=panel_send.at[q, c], recv_sem=panel_recv.at[q, c],
            device_id={"mode": above}, device_id_type=MESH)

    has_above = level < n_mode - 1
    top = n_mode - 1
    early = n_mode >= 3
    below = lax.rem(level + n_mode - 1, n_mode)

    def down_copy(c):
        return pltpu.make_async_remote_copy(
            src_ref=panels_ref.at[top, c], dst_ref=panels_ref.at[top, c],
            send_sem=down_send.at[c], recv_sem=down_recv.at[c],
            device_id={"mode": below}, device_id_type=MESH)

    def split(x):
        high = x.astype(BF16)
        return high, (x - high.astype(F32)).astype(BF16)

    gacc[...] = jnp.zeros_like(gacc)

    def second_group(i, carry):
        c = lax.rem(i + 1, groups)
        for half in range(GROUP):
            b = c * GROUP + half
            piece = (2.0 / filter_half * (image_of(window_b, b) - filter_center * first[b]) - start[b]) * live_of(b)
            own_ref[c, :, half * block:(half + 1) * block] = piece
        panels_ref[level, c] = own_ref[c].astype(BF16)

        @pl.when(has_above)
        def _():
            panel_copy(level, c).start()

        if early:
            @pl.when(level == top)
            def _():
                down_copy(c).start()

        high, low = split(own_ref[c])
        gacc[level] += nt_dot(high, high) + (nt_dot(high, low) + nt_dot(low, high))
        return carry

    for copy in halo_b:
        copy.wait_recv()
    lax.fori_loop(0, groups, second_group, 0)

    for d in range(1, n_mode):
        late = early and d == top

        @pl.when(level >= d)
        def _():
            q = lax.rem(level - d + n_mode, n_mode)

            def arrival(i, carry):
                c = lax.rem(i + 1, groups)
                panel_copy(q, c).wait_recv()

                @pl.when(has_above)
                def _():
                    panel_copy(q, c).start()

                high, low = split(own_ref[c])
                other = panels_ref[q, c]
                gacc[q] += nt_dot(high, other) + nt_dot(low, other)
                if early and d == top - 1:
                    @pl.when(level == top - 1)
                    def _():
                        down_copy(c).wait_recv()
                        gacc[n_mode] += nt_dot(panels_ref[top, c], other)
                return carry

            if not late:
                lax.fori_loop(0, groups, arrival, 0)

    for q in range(n_mode + 1):
        for s in range(n_space):
            gsend[s, :, q * panel_size:(q + 1) * panel_size] = gacc[q, s * share:(s + 1) * share, :]

    def rs_copy(target, slot):
        return pltpu.make_async_remote_copy(
            src_ref=gsend.at[target], dst_ref=grecv.at[slot],
            send_sem=rs_send.at[target], recv_sem=rs_recv.at[slot],
            device_id={"space": target}, device_id_type=MESH)

    for step in range(1, n_space):
        rs_copy(lax.rem(here + step, n_space), here).start()
    total = gsend[here]
    for step in range(1, n_space):
        peer = lax.rem(here + step, n_space)
        rs_copy(peer, peer).wait_recv()
        total = total + grecv[peer]
    gz[level] = total

    def z_copy(target, slot):
        return pltpu.make_async_remote_copy(
            src_ref=gz.at[slot], dst_ref=gz.at[slot],
            send_sem=z_send.at[target], recv_sem=z_recv.at[slot],
            device_id={"mode": target}, device_id_type=MESH)

    for step in range(1, n_mode):
        @pl.when(level + step < n_mode)
        def _():
            z_copy(lax.rem(level + step, n_mode), level).start()

    def ag_copy(target, origin, slot):
        return pltpu.make_async_remote_copy(
            src_ref=gz.at[slot], dst_ref=gram_ref.at[origin, slot],
            send_sem=ag_send.at[target, slot], recv_sem=ag_recv.at[origin, slot],
            device_id={"space": target}, device_id_type=MESH)

    def spread(slot):
        for step in range(1, n_space):
            ag_copy(lax.rem(here + step, n_space), here, slot).start()
        gram_ref[here, slot] = gz[slot]

    spread(level)
    for q in range(n_mode - 1):
        @pl.when(q < level)
        def _():
            z_copy(q, q).wait_recv()
            spread(q)

    for q in range(n_mode):
        @pl.when(q <= level)
        def _():
            for step in range(1, n_space):
                peer = lax.rem(here + step, n_space)
                ag_copy(peer, peer, q).wait_recv()
                ag_copy(peer, here, q).wait_send()

    if early:
        @pl.when(level == top)
        def _():
            def landed(i, carry):
                c = lax.rem(i + 1, groups)
                panel_copy(0, c).wait_recv()
                down_copy(c).wait_send()
                return carry

            lax.fori_loop(0, groups, landed, 0)

    for copy in halo_a:
        copy.wait_send()
    for copy in halo_b:
        copy.wait_send()
    for step in range(1, n_space):
        peer = lax.rem(here + step, n_space)
        rs_copy(peer, here).wait_send()
    for step in range(1, n_mode):
        @pl.when(level + step < n_mode)
        def _():
            z_copy(lax.rem(level + step, n_mode), level).wait_send()
    for d in range(n_mode):
        @pl.when(has_above & (level >= d))
        def _():
            q = lax.rem(level - d + n_mode, n_mode)

            def sent(c, carry):
                panel_copy(q, c).wait_send()
                return carry

            lax.fori_loop(0, groups, sent, 0)


def finish_kernel(gram_ref, own_hbm, panels_hbm, out_ref, scaled, inverse, extra, own_ref, panels_ref, load_sem):
    loads = (
        pltpu.make_async_copy(own_hbm, own_ref, load_sem.at[0]),
        pltpu.make_async_copy(panels_hbm, panels_ref, load_sem.at[1]),
    )
    for copy in loads:
        copy.start()
    n_mode, groups, panel_size, width = panels_ref.shape
    n_space, _, share, _ = gram_ref.shape
    size = n_mode * panel_size
    level = lax.axis_index("mode")
    for q in range(n_mode):
        for s in range(n_space):
            base = q * panel_size + s * share
            extra[base:base + share, :] = gram_ref[s, q, :, :size]

    if n_mode >= 3:
        @pl.when(level == n_mode - 1)
        def _():
            for s in range(n_space):
                base = size - panel_size + s * share
                extra[base:base + share, :panel_size] += gram_ref[s, n_mode - 2, :, size:]

    rows = lax.broadcasted_iota(jnp.int32, (size, size), 0)
    cols = lax.broadcasted_iota(jnp.int32, (size, size), 1)
    eye = (rows == cols).astype(F32)
    edge = (level + 1) * panel_size
    gram = jnp.where(rows < edge, extra[...], eye)
    gram = jnp.where(rows >= cols, gram, 0.0)
    diag_col = jnp.sum(jnp.where(rows == cols, gram, 0.0), axis=1, keepdims=True)
    diag_row = jnp.sum(jnp.where(rows == cols, gram, 0.0), axis=0, keepdims=True)
    scale_col = lax.rsqrt(diag_col)
    scale_row = lax.rsqrt(diag_row)
    lower = jnp.where(rows > cols, gram * scale_col * scale_row, 0.0)
    scaled[...] = lower + lower.T + eye

    def half_lower(error):
        return jnp.where(rows > cols, error, jnp.where(rows == cols, 0.5 * error, 0.0))

    x = eye - lower
    low_scaled = scaled[...].astype(BF16)
    for _ in range(2):
        low_x = x.astype(BF16)
        moved = jnp.dot(low_x, low_scaled, preferred_element_type=F32)
        error = nt_dot(moved.astype(BF16), low_x) - eye
        x = x - jnp.dot(half_lower(error).astype(BF16), low_x, preferred_element_type=F32)
    inverse[...] = x

    def split(a):
        high = a.astype(BF16)
        return high, (a - high.astype(F32)).astype(BF16)

    def dot3(a, b, product=functools.partial(jnp.dot, preferred_element_type=F32)):
        return product(a[0], b[0]) + (product(a[0], b[1]) + product(a[1], b[0]))

    def unfinished(state):
        step, worst = state
        return (worst > 1e-3) & (step < 12)

    def improve(state):
        step, _ = state
        x = inverse[...]
        parts = split(x)
        error = dot3(split(dot3(parts, split(scaled[...]))), parts, nt_dot) - eye
        worst = jnp.max(jnp.abs(error))
        inverse[...] = x - dot3(split(half_lower(error)), parts)
        return step + 1, jnp.where(worst < 1e30, worst, F32(1e30))

    _, worst = lax.while_loop(unfinished, improve, (0, F32(1.0)))

    @pl.when(jnp.logical_not(worst <= 1e-3))
    def _():
        inverse[...] = eye
        extra[...] = scaled[...]

        def eliminate(j, carry):
            pivot_row = extra[pl.ds(j, 1), :]
            pivot = jnp.sum(jnp.where(lax.broadcasted_iota(jnp.int32, (1, size), 1) == j, pivot_row, 0.0), axis=1, keepdims=True)
            x_row = inverse[pl.ds(j, 1), :]
            column = jnp.sum(jnp.where(cols == j, extra[...], 0.0), axis=1, keepdims=True)
            index = lax.broadcasted_iota(jnp.int32, (size, 1), 0)
            factor = jnp.where(index > j, column / pivot, 0.0)
            extra[...] = extra[...] - factor * pivot_row
            inverse[...] = inverse[...] - factor * x_row
            return carry

        lax.fori_loop(0, size, eliminate, 0)
        pivots = jnp.sum(jnp.where(rows == cols, extra[...], 0.0), axis=1, keepdims=True)
        inverse[...] = inverse[...] * lax.rsqrt(pivots)

    inverse[...] = inverse[...] * scale_row
    mine = inverse[pl.ds(pl.multiple_of(level * panel_size, panel_size), panel_size), :]
    for q in range(n_mode):
        part = mine[:, q * panel_size:(q + 1) * panel_size]

        @pl.when(q == level)
        def _():
            extra[:panel_size, :panel_size] = part

    for copy in loads:
        copy.wait()
    own_part = split(extra[:panel_size, :panel_size])
    for c in range(groups):
        out_ref[:, c * width:(c + 1) * width] = dot3(own_part, split(own_ref[c]))
    for q in range(n_mode - 1):
        @pl.when(q < level)
        def _():
            part = mine[:, q * panel_size:(q + 1) * panel_size].astype(BF16)
            for c in range(groups):
                out_ref[:, c * width:(c + 1) * width] += jnp.dot(part, panels_ref[q, c], preferred_element_type=F32)


def per_device(n_space, n_mode, start_modes, hessian, block_exponent, col_block, grain_count):
    panel_size, rows_here = start_modes.shape
    slab_blocks, contacts, block, _ = hessian.shape
    groups, width = slab_blocks // GROUP, GROUP * block
    share = panel_size // n_space
    modes = panel_size * n_mode
    window = slab_blocks + 2 * HALO_BLOCKS
    vmem = pl.BlockSpec(memory_space=pltpu.VMEM)
    smem = pl.BlockSpec(memory_space=pltpu.SMEM)
    hbm = pl.BlockSpec(memory_space=pl.ANY)
    dma = pltpu.SemaphoreType.DMA
    own, panels, gram = pl.pallas_call(
        functools.partial(filter_kernel, n_space, n_mode),
        out_shape=(
            jax.ShapeDtypeStruct((groups, panel_size, width), F32),
            jax.ShapeDtypeStruct((n_mode, groups, panel_size, width), BF16),
            jax.ShapeDtypeStruct((n_space, n_mode, share, modes + panel_size), F32),
        ),
        in_specs=[hbm, hbm, smem, vmem, hbm],
        out_specs=(vmem, vmem, vmem),
        scratch_shapes=[
            pltpu.SMEM((contacts, slab_blocks), jnp.int32),
            pltpu.SMEM((contacts, slab_blocks), jnp.int32),
            pltpu.VMEM(hessian.shape, BF16),
            pltpu.VMEM((slab_blocks, panel_size, block), F32),
            pltpu.VMEM((slab_blocks, panel_size, block), F32),
            pltpu.VMEM((window, panel_size, block), BF16),
            pltpu.VMEM((window, panel_size, block), BF16),
            pltpu.VMEM((n_mode + 1, panel_size, panel_size), F32),
            pltpu.VMEM((n_space, share, modes + panel_size), F32),
            pltpu.VMEM((n_space, share, modes + panel_size), F32),
            pltpu.VMEM((n_mode, share, modes + panel_size), F32),
            dma((2,)), dma((slab_blocks,)), dma((4,)), dma((4,)),
            dma((n_mode, groups)), dma((n_mode, groups)),
            dma((n_space,)), dma((n_space,)), dma((n_mode,)), dma((n_mode,)),
            dma((n_space, n_mode)), dma((n_space, n_mode)), dma((groups,)), dma((groups,)),
        ],
        compiler_params=pltpu.CompilerParams(collective_id=0, has_side_effects=True),
        name="filter",
    )(block_exponent.T, col_block.T, grain_count, start_modes, hessian)
    return pl.pallas_call(
        finish_kernel,
        out_shape=jax.ShapeDtypeStruct(start_modes.shape, F32),
        in_specs=[vmem, hbm, hbm],
        out_specs=vmem,
        scratch_shapes=[pltpu.VMEM((modes, modes), F32)] * 3 + [
            pltpu.VMEM(own.shape, F32),
            pltpu.VMEM(panels.shape, BF16),
            dma((2,)),
        ],
        name="finish",
    )(gram, own, panels)


def solution(mesh):
    return jax.shard_map(
        functools.partial(per_device, mesh.shape["space"], mesh.shape["mode"]),
        mesh=mesh,
        in_specs=(
            P("mode", "space"),
            P("space", None, None, None),
            P("space", None),
            P("space", None),
            P("space"),
        ),
        out_specs=P("mode", "space"),
        check_vma=False,
    )
```
